32 devices in a mesh: dp: 8 (over y, x, core), space: 4 (over z).
Axes of the slice: x: 2, y: 2, z: 4, core: 2. Of those that a mesh axis runs over, the one named last changes fastest.
Arguments:
- inputs: bfloat16 [8, 32, 48, 512], P('dp', 'space'), may hold values from -6 to 6
- pre_act: bfloat16 [8, 32, 48, 512], P('dp', 'space'), may hold values from -8 to 8
- grad_out: bfloat16 [8, 32, 48, 512], P('dp', 'space'), may hold values from -6 to 6
- w_first: bfloat16 [512, 3, 3, 512], P('dp'), may hold values from -0.09375 to 0.09375
- w_second: bfloat16 [512, 3, 3, 512], P('dp'), may hold values from -0.09375 to 0.09375
Outputs:
- input_grad: float32 [8, 32, 48, 512], P('dp', 'space')
- first_grad: float32 [512, 3, 3, 512], P('dp')
- second_grad: float32 [512, 3, 3, 512], P('dp')
The draws below stay inside these ranges and needn't reach their ends.
All inputs are finite; a program needn't handle non-finite values.
Results may differ from the reference program's by a relative error of at most 0.0029.
Values may be sent and summed in bfloat16 or wider, within the bound.
No kernel may reach another device: no remote copies, remote signals or barrier semaphores. Data moves between devices by JAX's collectives and lax.ppermute only.
A program may use at most 128 MiB of HBM per device.

```python
import jax
import jax.numpy as jnp
from jax import lax

C = 512
TILE_W = 48
IMAGES = 8
ROWS = 32


def strengthened(values, stream_key, source, target, parts, factor):
    def block_of(dim):
        return (jnp.arange(values.shape[dim]) // (values.shape[dim] // parts)).reshape((-1,) + (1,) * (values.ndim - 1 - dim))

    one_side = jax.random.permutation(stream_key, parts)[block_of(target)]
    far = (block_of(target) + parts // 2) % parts
    return jnp.where((block_of(source) == one_side) | (block_of(source) == far), factor * values, values)


def level_of(stream_key, shape, cuts, low, top_value):
    def one(position, blocks):
        draws = jax.random.uniform(jax.random.fold_in(jax.random.fold_in(stream_key, 6), position), (blocks,), jnp.float32, low / len(cuts), top_value / len(cuts))
        return jnp.repeat(jnp.exp(draws), shape[position] // blocks).reshape((-1,) + (1,) * (len(shape) - position - 1))

    loudness = one(*cuts[0])
    for cut in cuts[1:]:
        loudness = loudness * one(*cut)
    return loudness


def gaussian(key, shape, deviation, bound, cuts=(), dtype=jnp.bfloat16):
    factor_of = level_of(key, shape, cuts, -0.22, 0.18) if cuts else 1.0
    entries = jax.random.normal(key, shape, jnp.float32) * deviation * factor_of
    return jnp.minimum(jnp.maximum(entries, -bound), bound).astype(dtype)


def noise_with(rng, shape, spread, bound, split, heavy, held_as=jnp.bfloat16):
    result = spread * jax.random.normal(rng, shape, jnp.float32)
    if split:
        result = result * level_of(rng, shape, split, -0.22, 0.18)
    return jnp.clip(strengthened(result, jax.random.fold_in(rng, 3), *heavy), -bound, bound).astype(held_as)


def setup_inputs(seed: int = 0) -> dict:
    splits = jax.random.split(jax.random.key(seed), 6)
    return {
        "inputs": gaussian(splits[0], (IMAGES, ROWS, TILE_W, C), 1.0, 6.0, ((0, 8), (1, 4))),
        "pre_act": gaussian(splits[1], (IMAGES, ROWS, TILE_W, C), 2.0, 8.0, ((0, 8), (1, 4))),
        "grad_out": noise_with(splits[2], (IMAGES, ROWS, TILE_W, C), 1.0, 6.0, ((0, 8), (1, 4)), (0, 3, 8, 2.0)),
        "w_first": gaussian(splits[3], (C, 3, 3, C), (9 * C) ** -0.5, 0.09375, ((0, 8),)),
        "w_second": gaussian(splits[4], (C, 3, 3, C), (9 * C) ** -0.5, 0.09375, ((0, 8),)),
    }


def tap_stack(padded, height, width, flipped):
    pieces = []
    for row_tap in range(3):
        for col_tap in range(3):
            row_start = 2 - row_tap if flipped else row_tap
            col_start = 2 - col_tap if flipped else col_tap
            pieces.append(padded[..., row_start:row_start + height, col_start:col_start + width, :])
    stacked = jnp.stack(pieces, axis=-2)
    return stacked.reshape(-1, 9 * stacked.shape[-1])


def pad_image(field):
    return jnp.pad(field, ((1, 1), (1, 1), (0, 0)))


def reference(inputs, pre_act, grad_out, w_first, w_second):
    height = inputs.shape[1]
    width = inputs.shape[2]
    channels = inputs.shape[3]
    first_mat = jnp.transpose(w_first, (1, 2, 0, 3)).reshape(9 * channels, channels)
    second_mat = jnp.transpose(w_second, (1, 2, 0, 3)).reshape(9 * channels, channels)

    def one_image(carry, image):
        x_img, h_img, g_img = image
        h_flat = h_img.astype(jnp.float32).reshape(-1, channels)
        sigma = jax.nn.sigmoid(h_flat)
        act = (h_flat * sigma).astype(jnp.bfloat16).reshape(height, width, channels)
        act_taps = tap_stack(pad_image(act), height, width, False)
        g_flat = g_img.reshape(-1, channels)
        second_term = jnp.dot(g_flat.T, act_taps, preferred_element_type=jnp.float32)
        g_taps = tap_stack(pad_image(g_img), height, width, True)
        act_grad = jnp.dot(g_taps, second_mat, preferred_element_type=jnp.float32)
        pre_grad = (act_grad * (sigma * (1.0 + h_flat * (1.0 - sigma)))).astype(jnp.bfloat16)
        x_taps = tap_stack(pad_image(x_img), height, width, False)
        first_term = jnp.dot(pre_grad.T, x_taps, preferred_element_type=jnp.float32)
        grad_taps = tap_stack(pad_image(pre_grad.reshape(height, width, channels)), height, width, True)
        in_grad = jnp.dot(grad_taps, first_mat, preferred_element_type=jnp.float32)
        in_grad = in_grad.reshape(height, width, channels)
        return (carry[0] + first_term, carry[1] + second_term), in_grad

    zeros = jnp.zeros((channels, 9 * channels), jnp.float32)
    totals, input_grad = lax.scan(one_image, (zeros, zeros), (inputs, pre_act, grad_out))
    first_grad = totals[0].reshape(channels, 3, 3, channels)
    second_grad = totals[1].reshape(channels, 3, 3, channels)
    return (input_grad, first_grad, second_grad)
```

```python
import jax
import jax.numpy as jnp
from jax import lax
from jax.experimental import pallas as pl
from jax.experimental.pallas import tpu as pltpu
from jax.sharding import PartitionSpec as P

BF = jnp.bfloat16
F32 = jnp.float32
PARAMS = pltpu.CompilerParams(vmem_limit_bytes=48 * 1024 * 1024)
ANY = pl.BlockSpec(memory_space=pl.ANY)
VM = pl.BlockSpec(memory_space=pltpu.VMEM)
SM = pl.BlockSpec(memory_space=pltpu.SMEM)


def xor_pairs(count, k):
    return [(i, i ^ k) for i in range(count)]


def swap(value, axis, k):
    return lax.ppermute(value, axis, xor_pairs(lax.axis_size(axis), k))


def shifted(flat, width):
    rows = flat.shape[0]
    wide = flat.astype(F32)
    col = lax.broadcasted_iota(jnp.int32, wide.shape, 0) % width
    left = jnp.where(col == 0, 0.0, pltpu.roll(wide, 1, 0)).astype(BF)
    right = jnp.where(col == width - 1, 0.0, pltpu.roll(wide, rows - 1, 0)).astype(BF)
    return left, flat, right


def conv_kernel(count, width, pieces, owned, gated):
    def body(*refs):
        ids = refs[0]
        up, mid, down = refs[1:4]
        weights = refs[4 : 4 + count]
        at = 4 + count
        if gated:
            pre = refs[at]
            at += 1
        out = refs[at]
        at += 1
        parts = refs[at : at + pieces]
        at += pieces
        field, kernel, sems = refs[at : at + 3]
        stage = refs[at + 3] if pieces else None
        copies = []
        for k in range(count):
            rows = weights[k].shape[0]
            start = pl.multiple_of((ids[0] ^ k) * rows, rows) if count > 1 else 0
            copies.append(
                pltpu.make_async_copy(weights[k], kernel.at[pl.ds(start, rows)], sems.at[k])
            )
            copies[-1].start()
        n = mid.shape[0]
        flat = jnp.concatenate([up[...], mid[...], down[...]], axis=0)
        left, same, right = shifted(flat, width)
        field[0] = right
        field[1] = same
        field[2] = left
        for copy in copies:
            copy.wait()
        c = out.shape[1]
        acc = None
        for r in range(3):
            for s in range(3):
                tap = 3 * r + s
                lhs = field[s, (2 - r) * width : (2 - r) * width + n, :]
                part = jnp.dot(
                    lhs, kernel[:, tap * c : (tap + 1) * c], preferred_element_type=F32
                )
                acc = part if acc is None else acc + part
        if gated:
            h = pre[...].astype(F32)
            sig = jax.nn.sigmoid(h)
            acc = acc * (sig * (1.0 + h * (1.0 - sig)))
        res = acc.astype(out.dtype)
        out[...] = res
        if pieces:
            w = c // pieces
            for t in range(pieces):
                stage[t] = res[:, t * w : (t + 1) * w]
            for k in range(pieces):
                parts[k][...] = stage[(ids[0] >> 1) ^ k]

    return body


def conv(ids, up, mid, down, weights, width, pre=None, pieces=0):
    n, c = mid.shape
    count = len(weights)
    owned = weights[0].shape[0]
    out_type = BF if pre is not None else F32
    outs = [jax.ShapeDtypeStruct((n, c), out_type)]
    scratch = [
        pltpu.VMEM((3, n + 2 * width, c), BF),
        pltpu.VMEM((owned * count, weights[0].shape[1]), BF),
        pltpu.SemaphoreType.DMA((count,)),
    ]
    if pieces:
        outs += [jax.ShapeDtypeStruct((n, c // pieces), BF)] * pieces
        scratch.append(pltpu.VMEM((pieces, n, c // pieces), BF))
    args = [ids, up, mid, down, *weights] + ([pre] if pre is not None else [])
    specs = [SM, VM, VM, VM] + [ANY] * count + ([VM] if pre is not None else [])
    return pl.pallas_call(
        conv_kernel(count, width, pieces, owned, pre is not None),
        out_shape=outs,
        in_specs=specs,
        out_specs=[VM] * len(outs),
        scratch_shapes=scratch,
        compiler_params=PARAMS,
        name="conv_gated" if pre is not None else "conv_plain",
    )(*args)


def wgrad_kernel(count, width):
    def body(*refs):
        ids = refs[0]
        fields = refs[1 : 1 + count]
        cots = refs[1 + count : 1 + 2 * count]
        keep, send = refs[1 + 2 * count : 3 + 2 * count]
        taps, cot, acc = refs[3 + 2 * count :]
        n = cots[0].shape[0]
        for i in range(count):
            left, same, right = shifted(fields[i][...], width)
            taps[i, 0] = left
            taps[i, 1] = same
            taps[i, 2] = right
            cot[:, i * n : (i + 1) * n] = cots[i][...].T
        c = fields[0].shape[1]
        for r in range(3):
            for s in range(3):
                total = None
                for i in range(count):
                    part = jnp.dot(
                        cot[:, i * n : (i + 1) * n],
                        taps[i, s, r * width : r * width + n, :],
                        preferred_element_type=F32,
                    )
                    total = part if total is None else total + part
                acc[:, (3 * r + s) * c : (3 * r + s + 1) * c] = total
        half = keep.shape[0]
        mine = ids[0] & 1
        keep[...] = acc[pl.ds(pl.multiple_of(mine * half, half), half), :]
        send[...] = acc[pl.ds(pl.multiple_of((1 - mine) * half, half), half), :]

    return body


def wgrad(ids, fields, cots, width):
    count = len(fields)
    n, w = cots[0].shape
    rows, c = fields[0].shape
    half = jax.ShapeDtypeStruct((w // 2, 9 * c), F32)
    return pl.pallas_call(
        wgrad_kernel(count, width),
        out_shape=[half, half],
        in_specs=[SM] + [VM] * (2 * count),
        out_specs=[VM, VM],
        scratch_shapes=[
            pltpu.VMEM((count, 3, rows, c), BF),
            pltpu.VMEM((w, count * n), BF),
            pltpu.VMEM((w, 9 * c), F32),
        ],
        compiler_params=PARAMS,
        name="wgrad",
    )(ids, *fields, *cots)


def reduced(keep, send):
    total = keep + swap(send, "dp", 1)
    count = lax.axis_size("space")
    at = lax.axis_index("space")
    blocks = total.reshape(count, total.shape[0] // count, total.shape[1])
    mine = lax.dynamic_index_in_dim(blocks, at, 0, keepdims=False)
    for k in range(1, count):
        sent = lax.dynamic_index_in_dim(blocks, at ^ k, 0, keepdims=False).astype(BF)
        mine = mine + swap(sent, "space", k).astype(F32)
    mine = mine.astype(BF)
    got = jnp.stack([mine] + [swap(mine, "space", k) for k in range(1, count)])
    order = jnp.arange(count) ^ at
    whole = jnp.concatenate(
        [lax.dynamic_index_in_dim(got, order[j], 0, keepdims=False) for j in range(count)], axis=0
    )
    return whole.astype(F32)


def per_device(inputs, pre_act, grad_out, w_first, w_second):
    _, height, width, c = inputs.shape
    n = height * width
    dp = lax.axis_size("dp")
    chips = dp // 2
    owned = w_first.shape[0]
    me = lax.axis_index("dp")
    ids = me.astype(jnp.int32).reshape(1)
    chip = me >> 1

    x = inputs.reshape(n, c)
    h = pre_act.reshape(n, c)
    g = grad_out.reshape(n, c)
    hf = h.astype(F32)
    act = (hf * jax.nn.sigmoid(hf)).astype(BF)

    w2 = w_second.reshape(owned, 9 * c)
    w1 = w_first.reshape(owned, 9 * c)
    w1_all = lax.all_gather(w1, "dp", axis=0, tiled=True)

    strips = lax.axis_size("space")
    down_pairs = [(i, i + 1) for i in range(strips - 1)]
    up_pairs = [(i + 1, i) for i in range(strips - 1)]

    def halos(value):
        above = lax.ppermute(value[..., n - width :, :], "space", down_pairs)
        below = lax.ppermute(value[..., :width, :], "space", up_pairs)
        return above, below

    above, below = halos(jnp.stack([x, act, g]))
    x_ext = jnp.concatenate([above[0], x, below[0]], axis=0)
    act_ext = jnp.concatenate([above[1], act, below[1]], axis=0)

    shards = [w2] + [None] * (dp - 1)
    for k in range(2, dp, 2):
        shards[k] = swap(w2, "dp", k)
    for k in range(0, dp, 2):
        shards[k + 1] = swap(shards[k], "dp", 1)

    pre_grad, *cots = conv(ids, above[2], g, below[2], shards, width, pre=h, pieces=chips)

    acts = [act_ext] + [swap(act_ext, "dp", 2 * k) for k in range(1, chips)]
    block = g.reshape(n, chips, c // chips)
    g_cots = []
    for k in range(chips):
        part = lax.dynamic_index_in_dim(block, chip ^ k, 1, keepdims=False)
        g_cots.append(swap(part, "dp", 2 * k) if k else part)
    second = reduced(*wgrad(ids, acts, g_cots, width))

    xs = [x_ext] + [swap(x_ext, "dp", 2 * k) for k in range(1, chips)]
    p_cots = [cots[0]] + [swap(cots[k], "dp", 2 * k) for k in range(1, chips)]
    first = reduced(*wgrad(ids, xs, p_cots, width))

    p_above, p_below = halos(pre_grad)
    (in_grad,) = conv(ids, p_above, pre_grad, p_below, [w1_all], width)
    shape = (owned, 3, 3, c)
    return in_grad.reshape(inputs.shape), first.reshape(shape), second.reshape(shape)


def solution(mesh):
    return jax.shard_map(
        per_device,
        mesh=mesh,
        in_specs=(
            P("dp", "space", None, None),
            P("dp", "space", None, None),
            P("dp", "space", None, None),
            P("dp", None, None, None),
            P("dp", None, None, None),
        ),
        out_specs=(
            P("dp", "space", None, None),
            P("dp", None, None, None),
            P("dp", None, None, None),
        ),
        check_vma=False,
    )
```

```python
import jax
import jax.numpy as jnp
from jax import lax
from jax.experimental import pallas as pl
from jax.experimental.pallas import tpu as pltpu
from jax.sharding import PartitionSpec as P

BF = jnp.bfloat16
F32 = jnp.float32
PARAMS = pltpu.CompilerParams(vmem_limit_bytes=48 * 1024 * 1024)
ANY = pl.BlockSpec(memory_space=pl.ANY)
VM = pl.BlockSpec(memory_space=pltpu.VMEM)
SM = pl.BlockSpec(memory_space=pltpu.SMEM)


def xor_pairs(count, k):
    return [(i, i ^ k) for i in range(count)]


def swap(value, axis, k):
    return lax.ppermute(value, axis, xor_pairs(lax.axis_size(axis), k))


def shifted(flat, width):
    rows = flat.shape[0]
    wide = flat.astype(F32)
    col = lax.broadcasted_iota(jnp.int32, wide.shape, 0) % width
    left = jnp.where(col == 0, 0.0, pltpu.roll(wide, 1, 0)).astype(BF)
    right = jnp.where(col == width - 1, 0.0, pltpu.roll(wide, rows - 1, 0)).astype(BF)
    return left, flat, right


def products(field, kernel, n, c, width):
    acc = None
    for r in range(3):
        for s in range(3):
            tap = 3 * r + s
            lhs = field[s, (2 - r) * width : (2 - r) * width + n, :]
            part = jnp.dot(lhs, kernel[:, tap * c : (tap + 1) * c], preferred_element_type=F32)
            acc = part if acc is None else acc + part
    return acc


def gated_kernel(count, width, pieces):
    def body(*refs):
        ids, gup, g, gdown, hup, h, hdown = refs[:7]
        weights = refs[7 : 7 + count]
        out, parts, field, kernel, sems = refs[7 + count :]
        copies = []
        for k in range(count):
            rows = weights[k].shape[0]
            start = pl.multiple_of((ids[0] ^ k) * rows, rows)
            copies.append(
                pltpu.make_async_copy(weights[k], kernel.at[pl.ds(start, rows)], sems.at[k])
            )
            copies[-1].start()
        left, same, right = shifted(
            jnp.concatenate([gup[...], g[...], gdown[...]], axis=0), width
        )
        field[0] = right
        field[1] = same
        field[2] = left
        for copy in copies:
            copy.wait()
        n, c = out.shape
        acc = products(field, kernel, n, c, width)
        hf = jnp.concatenate([hup[...], h[...], hdown[...]], axis=0).astype(F32)
        sig = jax.nn.sigmoid(hf)
        acc = acc * (sig * (1.0 + hf * (1.0 - sig)))
        row = lax.broadcasted_iota(jnp.int32, acc.shape, 0)
        inside = jnp.logical_and(
            jnp.logical_or(row >= width, ids[1] > 0),
            jnp.logical_or(row < n - width, ids[2] > 0),
        )
        res = jnp.where(inside, acc, 0.0).astype(BF)
        out[...] = res
        w = c // pieces
        for t in range(pieces):
            parts[t] = res[:, t * w : (t + 1) * w]

    return body


def gated(ids, gup, g, gdown, hup, h, hdown, weights, width, pieces):
    n, c = h.shape
    count = len(weights)
    rows = n + 2 * width
    return pl.pallas_call(
        gated_kernel(count, width, pieces),
        out_shape=[
            jax.ShapeDtypeStruct((rows, c), BF),
            jax.ShapeDtypeStruct((pieces, rows, c // pieces), BF),
        ],
        in_specs=[SM] + [VM] * 6 + [ANY] * count,
        out_specs=[VM, VM],
        scratch_shapes=[
            pltpu.VMEM((3, rows + 2 * width, c), BF),
            pltpu.VMEM((weights[0].shape[0] * count, weights[0].shape[1]), BF),
            pltpu.SemaphoreType.DMA((count,)),
        ],
        compiler_params=PARAMS,
        name="gated",
    )(ids, gup, g, gdown, hup, h, hdown, *weights)


def plain_kernel(width):
    def body(ext, weight, out, field):
        left, same, right = shifted(ext[...], width)
        field[0] = right
        field[1] = same
        field[2] = left
        n, c = out.shape
        out[...] = products(field, weight, n, c, width)

    return body


def plain(ext, weight, width):
    rows, c = ext.shape
    return pl.pallas_call(
        plain_kernel(width),
        out_shape=jax.ShapeDtypeStruct((rows - 2 * width, c), F32),
        in_specs=[VM, VM],
        out_specs=VM,
        scratch_shapes=[pltpu.VMEM((3, rows, c), BF)],
        compiler_params=PARAMS,
        name="plain",
    )(ext, weight)


def wgrad_kernel(width):
    def body(ids, fields, cots, keep, send, lhs, acc):
        count, rows, w = cots.shape
        n = rows - 2 * width
        for i in range(count):
            left, same, right = shifted(cots[i], width)
            for s, part in enumerate((right, same, left)):
                for r in range(3):
                    tap = 3 * r + s
                    lhs[tap * w : (tap + 1) * w, i * n : (i + 1) * n] = part[
                        (2 - r) * width : (2 - r) * width + n, :
                    ].T
        for tap in range(9):
            acc[tap] = jnp.dot(
                lhs[tap * w : (tap + 1) * w, :], fields[...], preferred_element_type=F32
            )
        half = w // 2
        mine = ids[0] & 1
        keep[...] = acc[:, pl.ds(pl.multiple_of(mine * half, half), half), :]
        send[...] = acc[:, pl.ds(pl.multiple_of((1 - mine) * half, half), half), :]

    return body


def wgrad(ids, fields, cots, width):
    count, _, w = cots.shape
    n, c = fields.shape
    half = jax.ShapeDtypeStruct((9, w // 2, c), F32)
    return pl.pallas_call(
        wgrad_kernel(width),
        out_shape=[half, half],
        in_specs=[SM, VM, VM],
        out_specs=[VM, VM],
        scratch_shapes=[pltpu.VMEM((9 * w, n), BF), pltpu.VMEM((9, w, c), F32)],
        compiler_params=PARAMS,
        name="wgrad",
    )(ids, fields, cots)


def reduced(keep, send):
    total = keep + swap(send, "dp", 1)
    owned, c = total.shape[1:]
    count = lax.axis_size("space")
    at = lax.axis_index("space")
    blocks = total.reshape(count, 9 * owned // count, c)
    got = lax.all_to_all(blocks.astype(BF), "space", 0, 0)
    own = (jnp.arange(count) == at)[:, None, None]
    mine = jnp.sum(jnp.where(own, blocks, got.astype(F32)), axis=0).astype(BF)
    whole = lax.all_to_all(jnp.broadcast_to(mine, (count,) + mine.shape), "space", 0, 0)
    whole = whole.reshape(3, 3, owned, c).transpose(2, 0, 1, 3)
    return whole.astype(F32)


def after(value, *others):
    return lax.optimization_barrier((value,) + others)[0]


def per_device(inputs, pre_act, grad_out, w_first, w_second):
    _, height, width, c = inputs.shape
    n = height * width
    dp = lax.axis_size("dp")
    chips = dp // 2
    owned = w_first.shape[0]
    me = lax.axis_index("dp")
    strips = lax.axis_size("space")
    at = lax.axis_index("space")
    ids = jnp.stack([me, at, strips - 1 - at]).astype(jnp.int32)
    same_core = [[2 * q + k for q in range(chips)] for k in range(2)]

    def exchange(blocks):
        return lax.all_to_all(blocks, "dp", 0, 0, axis_index_groups=same_core)

    x = inputs.reshape(n, c)
    h = pre_act.reshape(n, c)
    g = grad_out.reshape(n, c)
    hf = h.astype(F32)
    act = (hf * jax.nn.sigmoid(hf)).astype(BF)

    acts = lax.all_gather(act, "dp", axis=0, tiled=True, axis_index_groups=same_core)
    w1 = after(w_first.reshape(owned, 9 * c), acts)
    w1_all = lax.all_gather(w1, "dp", axis=0, tiled=True)

    down_pairs = [(i, i + 1) for i in range(strips - 1)]
    up_pairs = [(i + 1, i) for i in range(strips - 1)]
    tail = jnp.concatenate([g[n - 2 * width :], h[n - width :]], axis=0)
    head = jnp.concatenate([g[: 2 * width], h[:width]], axis=0)
    above = lax.ppermute(tail, "space", down_pairs)
    below = lax.ppermute(head, "space", up_pairs)
    gup, hup = above[: 2 * width], above[2 * width :]
    gdown, hdown = below[: 2 * width], below[2 * width :]

    w2 = w_second.reshape(owned, 9 * c)
    shards = [w2] + [None] * (dp - 1)
    for k in range(2, dp, 2):
        shards[k] = swap(w2, "dp", k)
    for k in range(0, dp, 2):
        shards[k + 1] = swap(shards[k], "dp", 1)

    g_ext = jnp.concatenate([gup[width:], g, gdown[:width]], axis=0)
    g_cots = exchange(g_ext.reshape(n + 2 * width, chips, c // chips).transpose(1, 0, 2))
    second = reduced(*wgrad(ids, acts, g_cots, width))

    x_late = after(x, *shards[2::2])
    xs = exchange(jnp.broadcast_to(x_late, (chips, n, c))).reshape(chips * n, c)

    pre_ext, pieces = gated(ids, gup, g, gdown, hup, h, hdown, shards, width, chips)
    first = reduced(*wgrad(ids, xs, exchange(pieces), width))

    in_grad = plain(pre_ext, w1_all, width)
    return in_grad.reshape(inputs.shape), first, second


def solution(mesh):
    return jax.shard_map(
        per_device,
        mesh=mesh,
        in_specs=(
            P("dp", "space", None, None),
            P("dp", "space", None, None),
            P("dp", "space", None, None),
            P("dp", None, None, None),
            P("dp", None, None, None),
        ),
        out_specs=(
            P("dp", "space", None, None),
            P("dp", None, None, None),
            P("dp", None, None, None),
        ),
        check_vma=False,
    )
```

```python
import jax
import jax.numpy as jnp
from jax import lax
from jax.experimental import pallas as pl
from jax.experimental.pallas import tpu as pltpu
from jax.sharding import PartitionSpec as P

BF = jnp.bfloat16
F32 = jnp.float32
PARAMS = pltpu.CompilerParams(vmem_limit_bytes=48 * 1024 * 1024)
ANY = pl.BlockSpec(memory_space=pl.ANY)
VM = pl.BlockSpec(memory_space=pltpu.VMEM)
SM = pl.BlockSpec(memory_space=pltpu.SMEM)


def xor_pairs(count, k):
    return [(i, i ^ k) for i in range(count)]


def swap(value, axis, k):
    return lax.ppermute(value, axis, xor_pairs(lax.axis_size(axis), k))


def shifted(flat, width):
    rows = flat.shape[0]
    wide = flat.astype(F32)
    col = lax.broadcasted_iota(jnp.int32, wide.shape, 0) % width
    left = jnp.where(col == 0, 0.0, pltpu.roll(wide, 1, 0)).astype(BF)
    right = jnp.where(col == width - 1, 0.0, pltpu.roll(wide, rows - 1, 0)).astype(BF)
    return left, flat, right


def products(field, kernel, n, c, width):
    acc = None
    for r in range(3):
        for s in range(3):
            tap = 3 * r + s
            lhs = field[s, (2 - r) * width : (2 - r) * width + n, :]
            part = jnp.dot(lhs, kernel[:, tap * c : (tap + 1) * c], preferred_element_type=F32)
            acc = part if acc is None else acc + part
    return acc


def weight_copies(ids, weights, kernel, sems):
    copies = []
    for k, weight in enumerate(weights):
        rows = weight.shape[0]
        start = pl.multiple_of((ids[0] ^ k) * rows, rows)
        copies.append(pltpu.make_async_copy(weight, kernel.at[pl.ds(start, rows)], sems.at[k]))
        copies[-1].start()
    return copies


def gated_kernel(count, width):
    def body(*refs):
        ids, gup, g, gdown, hup, h, hdown = refs[:7]
        weights = refs[7 : 7 + count]
        out, parts, field, kernel, sems = refs[7 + count :]
        copies = weight_copies(ids, weights, kernel, sems)
        left, same, right = shifted(
            jnp.concatenate([gup[...], g[...], gdown[...]], axis=0), width
        )
        field[0] = right
        field[1] = same
        field[2] = left
        for copy in copies:
            copy.wait()
        n, c = out.shape
        acc = products(field, kernel, n, c, width)
        hf = jnp.concatenate([hup[...], h[...], hdown[...]], axis=0).astype(F32)
        sig = jax.nn.sigmoid(hf)
        acc = acc * (sig * (1.0 + hf * (1.0 - sig)))
        row = lax.broadcasted_iota(jnp.int32, acc.shape, 0)
        inside = jnp.logical_and(
            jnp.logical_or(row >= width, ids[1] > 0),
            jnp.logical_or(row < n - width, ids[2] > 0),
        )
        res = jnp.where(inside, acc, 0.0).astype(BF)
        out[...] = res
        strips = parts.shape[0]
        each = c // (strips * count)
        src = lax.broadcasted_iota(jnp.int32, (c, c), 0)
        dst = lax.broadcasted_iota(jnp.int32, (c, c), 1)
        owner, rest = src // (strips * each), src % (strips * each)
        goes = (rest // each) * (count * each) + owner * each + rest % each
        moved = jnp.dot(
            res[width : n - width], (goes == dst).astype(BF), preferred_element_type=F32
        ).astype(BF)
        w = c // strips
        for t in range(strips):
            parts[t] = moved[:, t * w : (t + 1) * w]

    return body


def gated(ids, gup, g, gdown, hup, h, hdown, weights, width, pieces):
    n, c = h.shape
    count = len(weights)
    rows = n + 2 * width
    return pl.pallas_call(
        gated_kernel(count, width),
        out_shape=[
            jax.ShapeDtypeStruct((rows, c), BF),
            jax.ShapeDtypeStruct((pieces, n, c // pieces), BF),
        ],
        in_specs=[SM] + [VM] * 6 + [ANY] * count,
        out_specs=[VM, VM],
        scratch_shapes=[
            pltpu.VMEM((3, rows + 2 * width, c), BF),
            pltpu.VMEM((weights[0].shape[0] * count, weights[0].shape[1]), BF),
            pltpu.SemaphoreType.DMA((count,)),
        ],
        compiler_params=PARAMS,
        name="gated",
    )(ids, gup, g, gdown, hup, h, hdown, *weights)


def plain_kernel(count, width):
    def body(*refs):
        ids, ext = refs[:2]
        weights = refs[2 : 2 + count]
        out, field, kernel, sems = refs[2 + count :]
        copies = weight_copies(ids, weights, kernel, sems)
        left, same, right = shifted(ext[...], width)
        field[0] = right
        field[1] = same
        field[2] = left
        for copy in copies:
            copy.wait()
        n, c = out.shape
        out[...] = products(field, kernel, n, c, width)

    return body


def plain(ids, ext, weights, width):
    rows, c = ext.shape
    count = len(weights)
    return pl.pallas_call(
        plain_kernel(count, width),
        out_shape=jax.ShapeDtypeStruct((rows - 2 * width, c), F32),
        in_specs=[SM, VM] + [ANY] * count,
        out_specs=VM,
        scratch_shapes=[
            pltpu.VMEM((3, rows, c), BF),
            pltpu.VMEM((weights[0].shape[0] * count, weights[0].shape[1]), BF),
            pltpu.SemaphoreType.DMA((count,)),
        ],
        compiler_params=PARAMS,
        name="plain",
    )(ids, ext, *weights)


def wgrad_products(lhs, cots, fields, acc, width):
    w = cots[0].shape[1]
    n = cots[0].shape[0] - 2 * width
    for i, cot in enumerate(cots):
        left, same, right = shifted(cot, width)
        for s, part in enumerate((right, same, left)):
            for r in range(3):
                tap = 3 * r + s
                lhs[tap * w : (tap + 1) * w, i * n : (i + 1) * n] = part[
                    (2 - r) * width : (2 - r) * width + n, :
                ].T
    for tap in range(9):
        total = None
        for i, field in enumerate(fields):
            part = jnp.dot(
                lhs[tap * w : (tap + 1) * w, i * n : (i + 1) * n],
                field[...],
                preferred_element_type=F32,
            )
            total = part if total is None else total + part
        acc[tap] = total


def strip_kernel(count, width):
    def body(*refs):
        ids = refs[0]
        fields = refs[1 : 1 + count]
        cots = refs[1 + count : 1 + 2 * count]
        keep, send, lhs, acc = refs[1 + 2 * count :]
        wgrad_products(lhs, [cot[...] for cot in cots], fields, acc, width)
        half = keep.shape[1]
        mine = ids[0] & 1
        keep[...] = acc[:, pl.ds(pl.multiple_of(mine * half, half), half), :]
        send[...] = acc[:, pl.ds(pl.multiple_of((1 - mine) * half, half), half), :]

    return body


def strip_wgrad(ids, fields, cots, width):
    count = len(fields)
    n, c = fields[0].shape
    w = cots[0].shape[1]
    half = jax.ShapeDtypeStruct((9, w // 2, c), F32)
    return pl.pallas_call(
        strip_kernel(count, width),
        out_shape=[half, half],
        in_specs=[SM] + [VM] * (2 * count),
        out_specs=[VM, VM],
        scratch_shapes=[pltpu.VMEM((9 * w, count * n), BF), pltpu.VMEM((9, w, c), F32)],
        compiler_params=PARAMS,
        name="strip_wgrad",
    )(ids, *fields, *cots)


def image_kernel(width):
    def body(ids, field, cots, own, parts, lhs, acc):
        count, n, w = cots.shape
        zero = jnp.zeros((width, w), BF)
        cot = jnp.concatenate([zero] + [cots[t] for t in range(count)] + [zero], axis=0)
        wgrad_products(lhs, [cot], [field], acc, width)
        owners, _, each, _ = parts.shape
        for d in range(owners):
            block = acc[:, d * each : (d + 1) * each, :]
            parts[d] = block.astype(BF)

            @pl.when(ids[0] == d)
            def _():
                own[...] = block

    return body


def image_wgrad(ids, field, cots, owners, width):
    n, c = field.shape
    w = cots.shape[2]
    each = w // owners
    return pl.pallas_call(
        image_kernel(width),
        out_shape=[
            jax.ShapeDtypeStruct((9, each, c), F32),
            jax.ShapeDtypeStruct((owners, 9, each, c), BF),
        ],
        in_specs=[SM, VM, VM],
        out_specs=[VM, VM],
        scratch_shapes=[pltpu.VMEM((9 * w, n), BF), pltpu.VMEM((9, w, c), F32)],
        compiler_params=PARAMS,
        name="image_wgrad",
    )(ids, field, cots)


def strips_summed(keep, send):
    total = keep + swap(send, "dp", 1)
    owned, c = total.shape[1:]
    count = lax.axis_size("space")
    at = lax.axis_index("space")
    blocks = total.reshape(count, 9 * owned // count, c)
    mine = lax.dynamic_index_in_dim(blocks, at, 0, keepdims=False)
    for k in range(1, count):
        sent = lax.dynamic_index_in_dim(blocks, at ^ k, 0, keepdims=False).astype(BF)
        mine = mine + swap(sent, "space", k).astype(F32)
    mine = mine.astype(BF)
    got = jnp.stack([mine] + [swap(mine, "space", k) for k in range(1, count)])
    whole = jnp.concatenate(
        [lax.dynamic_index_in_dim(got, at ^ j, 0, keepdims=False) for j in range(count)], axis=0
    )
    whole = whole.reshape(3, 3, owned, c).transpose(2, 0, 1, 3)
    return whole.astype(F32)


def images_summed(own, parts):
    owners = parts.shape[0]
    got = lax.all_to_all(parts, "dp", 0, 0)
    here = (jnp.arange(owners) == lax.axis_index("dp"))[:, None, None, None]
    return jnp.sum(jnp.where(here, own, got.astype(F32)), axis=0).astype(BF)


def strips_shared(mine):
    count = lax.axis_size("space")
    whole = lax.all_to_all(jnp.broadcast_to(mine, (count,) + mine.shape), "space", 0, 0)
    _, taps, each, c = whole.shape
    whole = whole.transpose(0, 2, 1, 3).reshape(count * each, 3, 3, c)
    return whole.astype(F32)


def after(value, *others):
    return lax.optimization_barrier((value,) + others)[0]


def per_device(inputs, pre_act, grad_out, w_first, w_second):
    _, height, width, c = inputs.shape
    n = height * width
    dp = lax.axis_size("dp")
    chips = dp // 2
    owned = w_first.shape[0]
    me = lax.axis_index("dp")
    strips = lax.axis_size("space")
    at = lax.axis_index("space")
    ids = jnp.stack([me, at, strips - 1 - at]).astype(jnp.int32)

    def sent_to_chips(rows):
        return [swap(rows, "dp", k) for k in range(2, dp, 2)]

    def sent_to_pair(shards):
        return [shard for own in shards for shard in (own, swap(own, "dp", 1))]

    x = inputs.reshape(n, c)
    h = pre_act.reshape(n, c)
    g = grad_out.reshape(n, c)
    hf = h.astype(F32)
    act = (hf * jax.nn.sigmoid(hf)).astype(BF)

    w2 = w_second.reshape(owned, 9 * c)
    w2_shards = [w2] + sent_to_chips(w2)
    shards = sent_to_pair(w2_shards)

    down_pairs = [(i, i + 1) for i in range(strips - 1)]
    up_pairs = [(i + 1, i) for i in range(strips - 1)]
    tail = jnp.concatenate([g[n - 2 * width :], h[n - width :]], axis=0)
    head = jnp.concatenate([g[: 2 * width], h[:width]], axis=0)
    above = lax.ppermute(tail, "space", down_pairs)
    below = lax.ppermute(head, "space", up_pairs)
    gup, hup = above[: 2 * width], above[2 * width :]
    gdown, hdown = below[: 2 * width], below[2 * width :]

    x_late = after(x, above, below)
    image = lax.all_to_all(jnp.broadcast_to(x_late, (strips, n, c)), "space", 0, 0)
    image = image.reshape(strips * n, c)

    pre_ext, pieces = gated(ids, gup, g, gdown, hup, h, hdown, shards, width, strips)
    pieces = after(pieces, image)
    p_cots = lax.all_to_all(pieces, "space", 0, 0)

    g_ext = jnp.concatenate([gup[width:], g, gdown[:width]], axis=0)
    blocks = g_ext.reshape(n + 2 * width, chips, c // chips).transpose(1, 0, 2)
    act_late, blocks_late = after((act, blocks), *w2_shards[1:])
    acts, g_cots = [act], [lax.dynamic_index_in_dim(blocks, me >> 1, 0, keepdims=False)]
    for k in range(1, chips):
        acts.append(swap(act_late, "dp", 2 * k))
        part = lax.dynamic_index_in_dim(blocks_late, (me >> 1) ^ k, 0, keepdims=False)
        g_cots.append(swap(part, "dp", 2 * k))

    w1 = w_first.reshape(owned, 9 * c)
    w1_shards = [w1] + sent_to_chips(after(w1, *acts[1:], *g_cots[1:]))

    share = images_summed(*image_wgrad(ids, image, p_cots, dp, width))
    w1_shards = sent_to_pair(after(w1_shards, share))
    first = strips_shared(share)
    second = strips_summed(*strip_wgrad(ids, acts, g_cots, width))
    in_grad = plain(ids, pre_ext, w1_shards, width)
    return in_grad.reshape(inputs.shape), first, second


def solution(mesh):
    return jax.shard_map(
        per_device,
        mesh=mesh,
        in_specs=(
            P("dp", "space", None, None),
            P("dp", "space", None, None),
            P("dp", "space", None, None),
            P("dp", None, None, None),
            P("dp", None, None, None),
        ),
        out_specs=(
            P("dp", "space", None, None),
            P("dp", None, None, None),
            P("dp", None, None, None),
        ),
        check_vma=False,
    )
```

```python
import jax
import jax.numpy as jnp
from jax import lax
from jax.experimental import pallas as pl
from jax.experimental.pallas import tpu as pltpu
from jax.sharding import PartitionSpec as P

BF = jnp.bfloat16
F32 = jnp.float32
PARAMS = pltpu.CompilerParams(vmem_limit_bytes=48 * 1024 * 1024)
ANY = pl.BlockSpec(memory_space=pl.ANY)
VM = pl.BlockSpec(memory_space=pltpu.VMEM)
SM = pl.BlockSpec(memory_space=pltpu.SMEM)


def xor_pairs(count, k):
    return [(i, i ^ k) for i in range(count)]


def swap(value, axis, k):
    return lax.ppermute(value, axis, xor_pairs(lax.axis_size(axis), k))


def shifted(flat, width):
    rows = flat.shape[0]
    wide = flat.astype(F32)
    col = lax.broadcasted_iota(jnp.int32, wide.shape, 0) % width
    left = jnp.where(col == 0, 0.0, pltpu.roll(wide, 1, 0)).astype(BF)
    right = jnp.where(col == width - 1, 0.0, pltpu.roll(wide, rows - 1, 0)).astype(BF)
    return left, flat, right


def products(field, kernel, n, c, width):
    acc = None
    for r in range(3):
        for s in range(3):
            tap = 3 * r + s
            lhs = field[s, (2 - r) * width : (2 - r) * width + n, :]
            part = jnp.dot(lhs, kernel[:, tap * c : (tap + 1) * c], preferred_element_type=F32)
            acc = part if acc is None else acc + part
    return acc


def prep_kernel(owners, strips):
    def body(h, g, out):
        n, c = h.shape
        each = c // (strips * owners)
        src = lax.broadcasted_iota(jnp.int32, (c, c), 0)
        dst = lax.broadcasted_iota(jnp.int32, (c, c), 1)
        owner, rest = src // (strips * each), src % (strips * each)
        goes = (rest // each) * (owners * each) + owner * each + rest % each
        moved = jnp.dot(g[...], (goes == dst).astype(BF), preferred_element_type=F32).astype(BF)
        hf = h[...].astype(F32)
        act = (hf * jax.nn.sigmoid(hf)).astype(BF)
        w = c // strips
        for t in range(strips):
            out[t, :, :c] = act
            out[t, :, c:] = moved[:, t * w : (t + 1) * w]

    return body


def prepared(h, g, owners, strips):
    n, c = h.shape
    return pl.pallas_call(
        prep_kernel(owners, strips),
        out_shape=jax.ShapeDtypeStruct((strips, n, c + c // strips), BF),
        in_specs=[VM, VM],
        out_specs=VM,
        compiler_params=PARAMS,
        name="prepared",
    )(h, g)


def weight_copies(ids, weights, kernel, sems):
    copies = []
    for k, weight in enumerate(weights):
        rows = weight.shape[0]
        start = pl.multiple_of((ids[0] ^ k) * rows, rows)
        copies.append(pltpu.make_async_copy(weight, kernel.at[pl.ds(start, rows)], sems.at[k]))
        copies[-1].start()
    return copies


def gated_kernel(count, width):
    def body(*refs):
        ids, gup, g, gdown, hup, h, hdown = refs[:7]
        weights = refs[7 : 7 + count]
        out, parts, field, kernel, sems = refs[7 + count :]
        copies = weight_copies(ids, weights, kernel, sems)
        left, same, right = shifted(
            jnp.concatenate([gup[...], g[...], gdown[...]], axis=0), width
        )
        field[0] = right
        field[1] = same
        field[2] = left
        for copy in copies:
            copy.wait()
        n, c = out.shape
        acc = products(field, kernel, n, c, width)
        hf = jnp.concatenate([hup[...], h[...], hdown[...]], axis=0).astype(F32)
        sig = jax.nn.sigmoid(hf)
        acc = acc * (sig * (1.0 + hf * (1.0 - sig)))
        row = lax.broadcasted_iota(jnp.int32, acc.shape, 0)
        inside = jnp.logical_and(
            jnp.logical_or(row >= width, ids[1] > 0),
            jnp.logical_or(row < n - width, ids[2] > 0),
        )
        res = jnp.where(inside, acc, 0.0).astype(BF)
        out[...] = res
        chips = parts.shape[0]
        w = c // chips
        for t in range(chips):
            parts[t] = res[:, t * w : (t + 1) * w]

    return body


def gated(ids, gup, g, gdown, hup, h, hdown, weights, width, pieces):
    n, c = h.shape
    count = len(weights)
    rows = n + 2 * width
    return pl.pallas_call(
        gated_kernel(count, width),
        out_shape=[
            jax.ShapeDtypeStruct((rows, c), BF),
            jax.ShapeDtypeStruct((pieces, rows, c // pieces), BF),
        ],
        in_specs=[SM] + [VM] * 6 + [ANY] * count,
        out_specs=[VM, VM],
        scratch_shapes=[
            pltpu.VMEM((3, rows + 2 * width, c), BF),
            pltpu.VMEM((weights[0].shape[0] * count, weights[0].shape[1]), BF),
            pltpu.SemaphoreType.DMA((count,)),
        ],
        compiler_params=PARAMS,
        name="gated",
    )(ids, gup, g, gdown, hup, h, hdown, *weights)


def plain_kernel(count, width):
    def body(*refs):
        ids, ext = refs[:2]
        weights = refs[2 : 2 + count]
        out, field, kernel, sems = refs[2 + count :]
        copies = weight_copies(ids, weights, kernel, sems)
        left, same, right = shifted(ext[...], width)
        field[0] = right
        field[1] = same
        field[2] = left
        for copy in copies:
            copy.wait()
        n, c = out.shape
        out[...] = products(field, kernel, n, c, width)

    return body


def plain(ids, ext, weights, width):
    rows, c = ext.shape
    count = len(weights)
    return pl.pallas_call(
        plain_kernel(count, width),
        out_shape=jax.ShapeDtypeStruct((rows - 2 * width, c), F32),
        in_specs=[SM, VM] + [ANY] * count,
        out_specs=VM,
        scratch_shapes=[
            pltpu.VMEM((3, rows, c), BF),
            pltpu.VMEM((weights[0].shape[0] * count, weights[0].shape[1]), BF),
            pltpu.SemaphoreType.DMA((count,)),
        ],
        compiler_params=PARAMS,
        name="plain",
    )(ids, ext, *weights)


def wgrad_products(lhs, cots, fields, acc, width):
    w = cots[0].shape[1]
    n = cots[0].shape[0] - 2 * width
    for i, cot in enumerate(cots):
        left, same, right = shifted(cot, width)
        for s, part in enumerate((right, same, left)):
            for r in range(3):
                tap = 3 * r + s
                lhs[tap * w : (tap + 1) * w, i * n : (i + 1) * n] = part[
                    (2 - r) * width : (2 - r) * width + n, :
                ].T
    for tap in range(9):
        total = None
        for i, field in enumerate(fields):
            part = jnp.dot(
                lhs[tap * w : (tap + 1) * w, i * n : (i + 1) * n],
                field[...],
                preferred_element_type=F32,
            )
            total = part if total is None else total + part
        acc[tap] = total


def strip_kernel(count, width):
    def body(*refs):
        ids = refs[0]
        fields = refs[1 : 1 + count]
        cots = refs[1 + count : 1 + 2 * count]
        keep, send, lhs, acc = refs[1 + 2 * count :]
        wgrad_products(lhs, [cot[...] for cot in cots], fields, acc, width)
        half = keep.shape[1]
        mine = ids[0] & 1
        keep[...] = acc[:, pl.ds(pl.multiple_of(mine * half, half), half), :]
        send[...] = acc[:, pl.ds(pl.multiple_of((1 - mine) * half, half), half), :]

    return body


def strip_wgrad(ids, fields, cots, width):
    count = len(fields)
    n, c = fields[0].shape
    w = cots[0].shape[1]
    half = jax.ShapeDtypeStruct((9, w // 2, c), F32)
    return pl.pallas_call(
        strip_kernel(count, width),
        out_shape=[half, half],
        in_specs=[SM] + [VM] * (2 * count),
        out_specs=[VM, VM],
        scratch_shapes=[pltpu.VMEM((9 * w, count * n), BF), pltpu.VMEM((9, w, c), F32)],
        compiler_params=PARAMS,
        name="strip_wgrad",
    )(ids, *fields, *cots)


def image_kernel(width):
    def body(ids, image, own, parts, lhs, acc):
        count, n, _ = image.shape
        c = own.shape[2]
        zero = jnp.zeros((width, acc.shape[1]), BF)
        cot = jnp.concatenate([zero] + [image[t, :, c:] for t in range(count)] + [zero], axis=0)
        field = jnp.concatenate([image[t, :, :c] for t in range(count)], axis=0)
        wgrad_products(lhs, [cot], [field], acc, width)
        owners, _, each, _ = parts.shape
        for d in range(owners):
            block = acc[:, d * each : (d + 1) * each, :]
            parts[d] = block.astype(BF)

            @pl.when(ids[0] == d)
            def _():
                own[...] = block

    return body


def image_wgrad(ids, image, c, owners, width):
    count, n, wide = image.shape
    w = wide - c
    each = w // owners
    return pl.pallas_call(
        image_kernel(width),
        out_shape=[
            jax.ShapeDtypeStruct((9, each, c), F32),
            jax.ShapeDtypeStruct((owners, 9, each, c), BF),
        ],
        in_specs=[SM, VM],
        out_specs=[VM, VM],
        scratch_shapes=[pltpu.VMEM((9 * w, count * n), BF), pltpu.VMEM((9, w, c), F32)],
        compiler_params=PARAMS,
        name="image_wgrad",
    )(ids, image)


def strips_summed(keep, send):
    total = keep + swap(send, "dp", 1)
    owned, c = total.shape[1:]
    count = lax.axis_size("space")
    at = lax.axis_index("space")
    blocks = total.reshape(9, count, owned // count, c)
    mine = lax.dynamic_index_in_dim(blocks, at, 1, keepdims=False)
    for k in range(1, count):
        sent = lax.dynamic_index_in_dim(blocks, at ^ k, 1, keepdims=False).astype(BF)
        mine = mine + swap(sent, "space", k).astype(F32)
    return mine.astype(BF)


def strips_gathered(mine):
    count = lax.axis_size("space")
    at = lax.axis_index("space")
    _, each, c = mine.shape
    got = jnp.stack([mine] + [swap(mine, "space", k) for k in range(1, count)])
    whole = jnp.stack(
        [lax.dynamic_index_in_dim(got, at ^ j, 0, keepdims=False) for j in range(count)]
    )
    return whole.transpose(0, 2, 1, 3).reshape(count * each, 3, 3, c).astype(F32)


def images_summed(own, parts):
    owners = parts.shape[0]
    got = lax.all_to_all(parts, "dp", 0, 0)
    here = (jnp.arange(owners) == lax.axis_index("dp"))[:, None, None, None]
    return jnp.sum(jnp.where(here, own, got.astype(F32)), axis=0).astype(BF)


def strips_shared(mine):
    count = lax.axis_size("space")
    whole = lax.all_to_all(jnp.broadcast_to(mine, (count,) + mine.shape), "space", 0, 0)
    _, taps, each, c = whole.shape
    whole = whole.transpose(0, 2, 1, 3).reshape(count * each, 3, 3, c)
    return whole.astype(F32)


def after(value, *others):
    return lax.optimization_barrier((value,) + others)[0]


def per_device(inputs, pre_act, grad_out, w_first, w_second):
    _, height, width, c = inputs.shape
    n = height * width
    dp = lax.axis_size("dp")
    chips = dp // 2
    owned = w_first.shape[0]
    me = lax.axis_index("dp")
    strips = lax.axis_size("space")
    at = lax.axis_index("space")
    ids = jnp.stack([me, at, strips - 1 - at]).astype(jnp.int32)

    same_core = [[2 * q + k for q in range(chips)] for k in range(2)]

    def sent_to_chips(rows):
        return [swap(rows, "dp", k) for k in range(2, dp, 2)]

    def sent_to_pair(shards):
        return [shard for own in shards for shard in (own, swap(own, "dp", 1))]

    x = inputs.reshape(n, c)
    h = pre_act.reshape(n, c)
    g = grad_out.reshape(n, c)

    image = lax.all_to_all(prepared(h, g, dp, strips), "space", 0, 0)

    w2 = w_second.reshape(owned, 9 * c)
    w2_shards = [w2] + sent_to_chips(w2)
    down_pairs = [(i, i + 1) for i in range(strips - 1)]
    up_pairs = [(i + 1, i) for i in range(strips - 1)]
    tail = jnp.concatenate([g[n - 2 * width :], h[n - width :]], axis=0)
    head = jnp.concatenate([g[: 2 * width], h[:width]], axis=0)
    above = lax.ppermute(tail, "space", down_pairs)
    below = lax.ppermute(head, "space", up_pairs)
    w2_shards, above, below = lax.optimization_barrier((w2_shards, above, below))
    shards = sent_to_pair(w2_shards)
    gup, hup = above[: 2 * width], above[2 * width :]
    gdown, hdown = below[: 2 * width], below[2 * width :]

    xs = [x] + sent_to_chips(after(x, *w2_shards[1:]))

    pre_ext, pieces = gated(ids, gup, g, gdown, hup, h, hdown, shards, width, chips)
    pieces, image, xs = lax.optimization_barrier((pieces, image, xs))
    p_cots = lax.all_to_all(pieces, "dp", 0, 0, axis_index_groups=same_core)
    chip = me >> 1
    cots = [lax.dynamic_index_in_dim(p_cots, chip ^ k, 0, keepdims=False) for k in range(chips)]
    own, parts = image_wgrad(ids, image, c, dp, width)
    cots, own = lax.optimization_barrier((cots, own))
    mine = strips_summed(*strip_wgrad(ids, xs, cots, width))
    share = images_summed(own, after(parts, p_cots))

    w1 = w_first.reshape(owned, 9 * c)
    w1_shards = [w1] + sent_to_chips(after(w1, p_cots))
    w1_shards = sent_to_pair(after(w1_shards, mine))
    first = strips_gathered(mine)
    second = strips_shared(share)
    in_grad = plain(ids, pre_ext, w1_shards, width)
    return in_grad.reshape(inputs.shape), first, second


def solution(mesh):
    return jax.shard_map(
        per_device,
        mesh=mesh,
        in_specs=(
            P("dp", "space", None, None),
            P("dp", "space", None, None),
            P("dp", "space", None, None),
            P("dp", None, None, None),
            P("dp", None, None, None),
        ),
        out_specs=(
            P("dp", "space", None, None),
            P("dp", None, None, None),
            P("dp", None, None, None),
        ),
        check_vma=False,
    )
```

```python
import jax
import jax.numpy as jnp
from jax import lax
from jax.experimental import pallas as pl
from jax.experimental.pallas import tpu as pltpu
from jax.sharding import PartitionSpec as P

BF = jnp.bfloat16
F32 = jnp.float32
PARAMS = pltpu.CompilerParams(vmem_limit_bytes=48 * 1024 * 1024)
ANY = pl.BlockSpec(memory_space=pltpu.HBM)
VM = pl.BlockSpec(memory_space=pltpu.VMEM)
SM = pl.BlockSpec(memory_space=pltpu.SMEM)


def xor_pairs(count, k):
    return [(i, i ^ k) for i in range(count)]


def swap(value, axis, k):
    return lax.ppermute(value, axis, xor_pairs(lax.axis_size(axis), k))


def shifted(flat, width):
    rows = flat.shape[0]
    wide = flat.astype(F32)
    col = lax.broadcasted_iota(jnp.int32, wide.shape, 0) % width
    left = jnp.where(col == 0, 0.0, pltpu.roll(wide, 1, 0)).astype(BF)
    right = jnp.where(col == width - 1, 0.0, pltpu.roll(wide, rows - 1, 0)).astype(BF)
    return left, flat, right


def products(field, kernel, copies, n, c, width):
    acc = None
    for r in range(3):
        for copy in copies[r]:
            copy.wait()
        for s in range(3):
            tap = 3 * r + s
            lhs = field[s, (2 - r) * width : (2 - r) * width + n, :]
            part = jnp.dot(lhs, kernel[:, tap * c : (tap + 1) * c], preferred_element_type=F32)
            acc = part if acc is None else acc + part
    return acc


def in_hbm(arrays):
    return [pltpu.with_memory_space_constraint(array, pltpu.HBM) for array in arrays]


def prep_kernel(owners, strips):
    def body(h, g, out):
        n, c = h.shape
        each = c // (strips * owners)
        src = lax.broadcasted_iota(jnp.int32, (c, c), 0)
        dst = lax.broadcasted_iota(jnp.int32, (c, c), 1)
        owner, rest = src // (strips * each), src % (strips * each)
        goes = (rest // each) * (owners * each) + owner * each + rest % each
        moved = jnp.dot(g[...], (goes == dst).astype(BF), preferred_element_type=F32).astype(BF)
        hf = h[...].astype(F32)
        act = (hf * jax.nn.sigmoid(hf)).astype(BF)
        w = c // strips
        for t in range(strips):
            out[t, :, :c] = act
            out[t, :, c:] = moved[:, t * w : (t + 1) * w]

    return body


def prepared(h, g, owners, strips):
    n, c = h.shape
    return pl.pallas_call(
        prep_kernel(owners, strips),
        out_shape=jax.ShapeDtypeStruct((strips, n, c + c // strips), BF),
        in_specs=[VM, VM],
        out_specs=VM,
        compiler_params=PARAMS,
        name="prepared",
    )(h, g)


def weight_copies(ids, weights, kernel, sems):
    count = len(weights)
    rows, wide = weights[0].shape
    copies = []
    for r in range(3):
        cols = pl.ds(r * (wide // 3), wide // 3)
        for k, weight in enumerate(weights):
            start = pl.multiple_of((ids[0] ^ k) * rows, rows)
            copies.append(
                pltpu.make_async_copy(
                    weight.at[:, cols], kernel.at[pl.ds(start, rows), cols], sems.at[r * count + k]
                )
            )
            copies[-1].start()
    return [copies[r * count : (r + 1) * count] for r in range(3)]


def gated_kernel(count, width):
    def body(*refs):
        ids, gup, g, gdown, hup, h, hdown = refs[:7]
        weights = refs[7 : 7 + count]
        out, parts, field, kernel, sems = refs[7 + count :]
        copies = weight_copies(ids, weights, kernel, sems)
        left, same, right = shifted(
            jnp.concatenate([gup[...], g[...], gdown[...]], axis=0), width
        )
        field[0] = right
        field[1] = same
        field[2] = left
        n, c = out.shape
        acc = products(field, kernel, copies, n, c, width)
        hf = jnp.concatenate([hup[...], h[...], hdown[...]], axis=0).astype(F32)
        sig = jax.nn.sigmoid(hf)
        acc = acc * (sig * (1.0 + hf * (1.0 - sig)))
        row = lax.broadcasted_iota(jnp.int32, acc.shape, 0)
        inside = jnp.logical_and(
            jnp.logical_or(row >= width, ids[1] > 0),
            jnp.logical_or(row < n - width, ids[2] > 0),
        )
        res = jnp.where(inside, acc, 0.0).astype(BF)
        out[...] = res
        chips = parts.shape[0]
        w = c // chips
        for t in range(chips):
            parts[t] = res[:, t * w : (t + 1) * w]

    return body


def gated(ids, gup, g, gdown, hup, h, hdown, weights, width, pieces):
    n, c = h.shape
    count = len(weights)
    rows = n + 2 * width
    return pl.pallas_call(
        gated_kernel(count, width),
        out_shape=[
            jax.ShapeDtypeStruct((rows, c), BF),
            jax.ShapeDtypeStruct((pieces, rows, c // pieces), BF),
        ],
        in_specs=[SM] + [VM] * 6 + [ANY] * count,
        out_specs=[VM, VM],
        scratch_shapes=[
            pltpu.VMEM((3, rows + 2 * width, c), BF),
            pltpu.VMEM((weights[0].shape[0] * count, weights[0].shape[1]), BF),
            pltpu.SemaphoreType.DMA((3 * count,)),
        ],
        compiler_params=PARAMS,
        name="gated",
    )(ids, gup, g, gdown, hup, h, hdown, *in_hbm(weights))


def plain_kernel(count, width):
    def body(*refs):
        ids, ext = refs[:2]
        weights = refs[2 : 2 + count]
        out, field, kernel, sems = refs[2 + count :]
        copies = weight_copies(ids, weights, kernel, sems)
        left, same, right = shifted(ext[...], width)
        field[0] = right
        field[1] = same
        field[2] = left
        n, c = out.shape
        out[...] = products(field, kernel, copies, n, c, width)

    return body


def plain(ids, ext, weights, width):
    rows, c = ext.shape
    count = len(weights)
    return pl.pallas_call(
        plain_kernel(count, width),
        out_shape=jax.ShapeDtypeStruct((rows - 2 * width, c), F32),
        in_specs=[SM, VM] + [ANY] * count,
        out_specs=VM,
        scratch_shapes=[
            pltpu.VMEM((3, rows, c), BF),
            pltpu.VMEM((weights[0].shape[0] * count, weights[0].shape[1]), BF),
            pltpu.SemaphoreType.DMA((3 * count,)),
        ],
        compiler_params=PARAMS,
        name="plain",
    )(ids, ext, *in_hbm(weights))


def wgrad_products(lhs, cots, fields, acc, width):
    w = cots[0].shape[1]
    n = cots[0].shape[0] - 2 * width
    for i, cot in enumerate(cots):
        left, same, right = shifted(cot, width)
        for s, part in enumerate((right, same, left)):
            for r in range(3):
                tap = 3 * r + s
                lhs[tap * w : (tap + 1) * w, i * n : (i + 1) * n] = part[
                    (2 - r) * width : (2 - r) * width + n, :
                ].T
    for tap in range(9):
        total = None
        for i, field in enumerate(fields):
            part = jnp.dot(
                lhs[tap * w : (tap + 1) * w, i * n : (i + 1) * n],
                field[...],
                preferred_element_type=F32,
            )
            total = part if total is None else total + part
        acc[tap] = total


def strip_kernel(count, width):
    def body(*refs):
        ids = refs[0]
        fields = refs[1 : 1 + count]
        cots = refs[1 + count : 1 + 2 * count]
        keep, send, lhs, acc = refs[1 + 2 * count :]
        wgrad_products(lhs, [cot[...] for cot in cots], fields, acc, width)
        half = keep.shape[1]
        mine = ids[0] & 1
        keep[...] = acc[:, pl.ds(pl.multiple_of(mine * half, half), half), :]
        send[...] = acc[:, pl.ds(pl.multiple_of((1 - mine) * half, half), half), :]

    return body


def strip_wgrad(ids, fields, cots, width):
    count = len(fields)
    n, c = fields[0].shape
    w = cots[0].shape[1]
    half = jax.ShapeDtypeStruct((9, w // 2, c), F32)
    return pl.pallas_call(
        strip_kernel(count, width),
        out_shape=[half, half],
        in_specs=[SM] + [VM] * (2 * count),
        out_specs=[VM, VM],
        scratch_shapes=[pltpu.VMEM((9 * w, count * n), BF), pltpu.VMEM((9, w, c), F32)],
        compiler_params=PARAMS,
        name="strip_wgrad",
    )(ids, *fields, *cots)


def image_kernel(width):
    def body(ids, image, own, parts, lhs, acc):
        count, n, _ = image.shape
        c = own.shape[2]
        zero = jnp.zeros((width, acc.shape[1]), BF)
        cot = jnp.concatenate([zero] + [image[t, :, c:] for t in range(count)] + [zero], axis=0)
        field = jnp.concatenate([image[t, :, :c] for t in range(count)], axis=0)
        wgrad_products(lhs, [cot], [field], acc, width)
        owners, _, each, _ = parts.shape
        for d in range(owners):
            block = acc[:, d * each : (d + 1) * each, :]
            parts[d] = block.astype(BF)

            @pl.when(ids[0] == d)
            def _():
                own[...] = block

    return body


def image_wgrad(ids, image, c, owners, width):
    count, n, wide = image.shape
    w = wide - c
    each = w // owners
    return pl.pallas_call(
        image_kernel(width),
        out_shape=[
            jax.ShapeDtypeStruct((9, each, c), F32),
            jax.ShapeDtypeStruct((owners, 9, each, c), BF),
        ],
        in_specs=[SM, VM],
        out_specs=[VM, VM],
        scratch_shapes=[pltpu.VMEM((9 * w, count * n), BF), pltpu.VMEM((9, w, c), F32)],
        compiler_params=PARAMS,
        name="image_wgrad",
    )(ids, image)


def strips_summed(keep, send):
    total = keep + swap(send, "dp", 1)
    owned, c = total.shape[1:]
    count = lax.axis_size("space")
    at = lax.axis_index("space")
    blocks = total.reshape(9, count, owned // count, c)
    mine = lax.dynamic_index_in_dim(blocks, at, 1, keepdims=False)
    for k in range(1, count):
        sent = lax.dynamic_index_in_dim(blocks, at ^ k, 1, keepdims=False).astype(BF)
        mine = mine + swap(sent, "space", k).astype(F32)
    return mine.astype(BF)


def strips_gathered(mine):
    count = lax.axis_size("space")
    at = lax.axis_index("space")
    _, each, c = mine.shape
    got = jnp.stack([mine] + [swap(mine, "space", k) for k in range(1, count)])
    whole = jnp.stack(
        [lax.dynamic_index_in_dim(got, at ^ j, 0, keepdims=False) for j in range(count)]
    )
    return whole.transpose(0, 2, 1, 3).reshape(count * each, 3, 3, c).astype(F32)


def images_summed(own, parts):
    owners = parts.shape[0]
    got = lax.all_to_all(parts, "dp", 0, 0)
    here = (jnp.arange(owners) == lax.axis_index("dp"))[:, None, None, None]
    return jnp.sum(jnp.where(here, own, got.astype(F32)), axis=0).astype(BF)


def strips_shared(mine):
    count = lax.axis_size("space")
    whole = lax.all_to_all(jnp.broadcast_to(mine, (count,) + mine.shape), "space", 0, 0)
    _, taps, each, c = whole.shape
    whole = whole.transpose(0, 2, 1, 3).reshape(count * each, 3, 3, c)
    return whole.astype(F32)


def after(value, *others):
    return lax.optimization_barrier((value,) + others)[0]


def per_device(inputs, pre_act, grad_out, w_first, w_second):
    _, height, width, c = inputs.shape
    n = height * width
    dp = lax.axis_size("dp")
    chips = dp // 2
    owned = w_first.shape[0]
    me = lax.axis_index("dp")
    strips = lax.axis_size("space")
    at = lax.axis_index("space")
    ids = jnp.stack([me, at, strips - 1 - at]).astype(jnp.int32)

    same_core = [[2 * q + k for q in range(chips)] for k in range(2)]

    def sent_to_chips(rows):
        return [swap(rows, "dp", k) for k in range(2, dp, 2)]

    def sent_to_pair(shards):
        return [shard for own in shards for shard in (own, swap(own, "dp", 1))]

    x = inputs.reshape(n, c)
    h = pre_act.reshape(n, c)
    g = grad_out.reshape(n, c)

    w2 = w_second.reshape(owned, 9 * c)
    ready = prepared(h, g, dp, strips)

    down_pairs = [(i, i + 1) for i in range(strips - 1)]
    up_pairs = [(i + 1, i) for i in range(strips - 1)]
    tail = jnp.concatenate([g[n - 2 * width :], h[n - width :]], axis=0)
    head = jnp.concatenate([g[: 2 * width], h[:width]], axis=0)
    above = lax.ppermute(tail, "space", down_pairs)
    below = lax.ppermute(head, "space", up_pairs)
    w2, ready, above, below = lax.optimization_barrier((w2, ready, above, below))
    image = lax.all_to_all(ready, "space", 0, 0)
    w2_shards = lax.optimization_barrier([w2] + sent_to_chips(w2))
    shards = sent_to_pair(w2_shards)
    gup, hup = above[: 2 * width], above[2 * width :]
    gdown, hdown = below[: 2 * width], below[2 * width :]

    xs = [x] + sent_to_chips(after(x, *w2_shards[1:]))

    pre_ext, pieces = gated(ids, gup, g, gdown, hup, h, hdown, shards, width, chips)
    pieces, image = lax.optimization_barrier((pieces, image))
    image = after(image, *xs[1:])
    p_cots = lax.all_to_all(pieces, "dp", 0, 0, axis_index_groups=same_core)
    chip = me >> 1
    cots = [lax.dynamic_index_in_dim(p_cots, chip ^ k, 0, keepdims=False) for k in range(chips)]
    own, parts = image_wgrad(ids, image, c, dp, width)
    cots, own = lax.optimization_barrier((cots, own))
    mine = strips_summed(*strip_wgrad(ids, xs, cots, width))
    share = images_summed(own, after(parts, p_cots))

    w1 = w_first.reshape(owned, 9 * c)
    w1_shards = [w1] + sent_to_chips(after(w1, share))
    w1_shards = sent_to_pair(w1_shards)
    first = strips_gathered(mine)
    second = strips_shared(share)
    in_grad = plain(ids, pre_ext, w1_shards, width)
    return in_grad.reshape(inputs.shape), first, second


def solution(mesh):
    return jax.shard_map(
        per_device,
        mesh=mesh,
        in_specs=(
            P("dp", "space", None, None),
            P("dp", "space", None, None),
            P("dp", "space", None, None),
            P("dp", None, None, None),
            P("dp", None, None, None),
        ),
        out_specs=(
            P("dp", "space", None, None),
            P("dp", None, None, None),
            P("dp", None, None, None),
        ),
        check_vma=False,
    )
```

```python
import jax
import jax.numpy as jnp
from jax import lax
from jax.experimental import pallas as pl
from jax.experimental.pallas import tpu as pltpu
from jax.sharding import PartitionSpec as P

BF = jnp.bfloat16
F32 = jnp.float32
PARAMS = pltpu.CompilerParams(vmem_limit_bytes=48 * 1024 * 1024)
ANY = pl.BlockSpec(memory_space=pltpu.HBM)
VM = pl.BlockSpec(memory_space=pltpu.VMEM)
SM = pl.BlockSpec(memory_space=pltpu.SMEM)


def xor_pairs(count, k):
    return [(i, i ^ k) for i in range(count)]


def swap(value, axis, k):
    return lax.ppermute(value, axis, xor_pairs(lax.axis_size(axis), k))


def shifted(flat, width):
    rows = flat.shape[0]
    wide = flat.astype(F32)
    col = lax.broadcasted_iota(jnp.int32, wide.shape, 0) % width
    left = jnp.where(col == 0, 0.0, pltpu.roll(wide, 1, 0)).astype(BF)
    right = jnp.where(col == width - 1, 0.0, pltpu.roll(wide, rows - 1, 0)).astype(BF)
    return left, flat, right


def products(field, kernel, copies, n, c, width):
    acc = None
    for r in range(3):
        for copy in copies[r]:
            copy.wait()
        for s in range(3):
            tap = 3 * r + s
            lhs = field[s, (2 - r) * width : (2 - r) * width + n, :]
            part = jnp.dot(lhs, kernel[:, tap * c : (tap + 1) * c], preferred_element_type=F32)
            acc = part if acc is None else acc + part
    return acc


def in_hbm(arrays):
    return [pltpu.with_memory_space_constraint(array, pltpu.HBM) for array in arrays]


def prep_kernel(owners, strips):
    def body(h, g, out):
        n, c = h.shape
        each = c // (strips * owners)
        src = lax.broadcasted_iota(jnp.int32, (c, c), 0)
        dst = lax.broadcasted_iota(jnp.int32, (c, c), 1)
        owner, rest = src // (strips * each), src % (strips * each)
        goes = (rest // each) * (owners * each) + owner * each + rest % each
        moved = jnp.dot(g[...], (goes == dst).astype(BF), preferred_element_type=F32).astype(BF)
        hf = h[...].astype(F32)
        act = (hf * jax.nn.sigmoid(hf)).astype(BF)
        w = c // strips
        for t in range(strips):
            out[t, :, :c] = act
            out[t, :, c:] = moved[:, t * w : (t + 1) * w]

    return body


def prepared(h, g, owners, strips):
    n, c = h.shape
    return pl.pallas_call(
        prep_kernel(owners, strips),
        out_shape=jax.ShapeDtypeStruct((strips, n, c + c // strips), BF),
        in_specs=[VM, VM],
        out_specs=VM,
        compiler_params=PARAMS,
        name="prepared",
    )(h, g)


def weight_copies(ids, weights, kernel, sems):
    count = len(weights)
    rows, wide = weights[0].shape
    copies = []
    for r in range(3):
        cols = pl.ds(r * (wide // 3), wide // 3)
        for k, weight in enumerate(weights):
            start = pl.multiple_of((ids[0] ^ k) * rows, rows)
            copies.append(
                pltpu.make_async_copy(
                    weight.at[:, cols], kernel.at[pl.ds(start, rows), cols], sems.at[r * count + k]
                )
            )
            copies[-1].start()
    return [copies[r * count : (r + 1) * count] for r in range(3)]


def gated_kernel(count, width):
    def body(*refs):
        ids, gup, g, gdown, hup, h, hdown = refs[:7]
        weights = refs[7 : 7 + count]
        out, parts, field, kernel, sems = refs[7 + count :]
        copies = weight_copies(ids, weights, kernel, sems)
        left, same, right = shifted(
            jnp.concatenate([gup[...], g[...], gdown[...]], axis=0), width
        )
        field[0] = right
        field[1] = same
        field[2] = left
        n, c = out.shape
        acc = products(field, kernel, copies, n, c, width)
        hf = jnp.concatenate([hup[...], h[...], hdown[...]], axis=0).astype(F32)
        sig = jax.nn.sigmoid(hf)
        acc = acc * (sig * (1.0 + hf * (1.0 - sig)))
        row = lax.broadcasted_iota(jnp.int32, acc.shape, 0)
        inside = jnp.logical_and(
            jnp.logical_or(row >= width, ids[1] > 0),
            jnp.logical_or(row < n - width, ids[2] > 0),
        )
        res = jnp.where(inside, acc, 0.0).astype(BF)
        out[...] = res
        chips = parts.shape[0]
        w = c // chips
        for t in range(chips):
            parts[t] = res[:, t * w : (t + 1) * w]

    return body


def gated(ids, gup, g, gdown, hup, h, hdown, weights, width, pieces):
    n, c = h.shape
    count = len(weights)
    rows = n + 2 * width
    return pl.pallas_call(
        gated_kernel(count, width),
        out_shape=[
            jax.ShapeDtypeStruct((rows, c), BF),
            jax.ShapeDtypeStruct((pieces, rows, c // pieces), BF),
        ],
        in_specs=[SM] + [VM] * 6 + [ANY] * count,
        out_specs=[VM, VM],
        scratch_shapes=[
            pltpu.VMEM((3, rows + 2 * width, c), BF),
            pltpu.VMEM((weights[0].shape[0] * count, weights[0].shape[1]), BF),
            pltpu.SemaphoreType.DMA((3 * count,)),
        ],
        compiler_params=PARAMS,
        name="gated",
    )(ids, gup, g, gdown, hup, h, hdown, *in_hbm(weights))


def plain_kernel(count, width):
    def body(*refs):
        ids, ext = refs[:2]
        weights = refs[2 : 2 + count]
        out, field, kernel, sems = refs[2 + count :]
        copies = weight_copies(ids, weights, kernel, sems)
        left, same, right = shifted(ext[...], width)
        field[0] = right
        field[1] = same
        field[2] = left
        n, c = out.shape
        out[...] = products(field, kernel, copies, n, c, width)

    return body


def plain(ids, ext, weights, width):
    rows, c = ext.shape
    count = len(weights)
    return pl.pallas_call(
        plain_kernel(count, width),
        out_shape=jax.ShapeDtypeStruct((rows - 2 * width, c), F32),
        in_specs=[SM, VM] + [ANY] * count,
        out_specs=VM,
        scratch_shapes=[
            pltpu.VMEM((3, rows, c), BF),
            pltpu.VMEM((weights[0].shape[0] * count, weights[0].shape[1]), BF),
            pltpu.SemaphoreType.DMA((3 * count,)),
        ],
        compiler_params=PARAMS,
        name="plain",
    )(ids, ext, *in_hbm(weights))


def wgrad_products(lhs, cots, fields, acc, width):
    w = cots[0].shape[1]
    n = cots[0].shape[0] - 2 * width
    for i, cot in enumerate(cots):
        left, same, right = shifted(cot, width)
        for s, part in enumerate((right, same, left)):
            for r in range(3):
                tap = 3 * r + s
                lhs[tap * w : (tap + 1) * w, i * n : (i + 1) * n] = part[
                    (2 - r) * width : (2 - r) * width + n, :
                ].T
    for tap in range(9):
        total = None
        for i, field in enumerate(fields):
            part = jnp.dot(
                lhs[tap * w : (tap + 1) * w, i * n : (i + 1) * n],
                field[...],
                preferred_element_type=F32,
            )
            total = part if total is None else total + part
        acc[tap] = total


def strip_kernel(count, width):
    def body(*refs):
        ids = refs[0]
        fields = refs[1 : 1 + count]
        cots, keep, send, lhs, acc = refs[1 + count :]
        ordered = [cots[(ids[0] >> 1) ^ i] for i in range(count)]
        wgrad_products(lhs, ordered, fields, acc, width)
        half = keep.shape[1]
        mine = ids[0] & 1
        keep[...] = acc[:, pl.ds(pl.multiple_of(mine * half, half), half), :]
        send[...] = acc[:, pl.ds(pl.multiple_of((1 - mine) * half, half), half), :]

    return body


def strip_wgrad(ids, fields, cots, width):
    count = len(fields)
    n, c = fields[0].shape
    w = cots.shape[2]
    half = jax.ShapeDtypeStruct((9, w // 2, c), F32)
    return pl.pallas_call(
        strip_kernel(count, width),
        out_shape=[half, half],
        in_specs=[SM] + [VM] * (count + 1),
        out_specs=[VM, VM],
        scratch_shapes=[pltpu.VMEM((9 * w, count * n), BF), pltpu.VMEM((9, w, c), F32)],
        compiler_params=PARAMS,
        name="strip_wgrad",
    )(ids, *fields, cots)


def image_kernel(width):
    def body(ids, image, own, parts, lhs, acc):
        count, n, _ = image.shape
        c = own.shape[2]
        zero = jnp.zeros((width, acc.shape[1]), BF)
        cot = jnp.concatenate([zero] + [image[t, :, c:] for t in range(count)] + [zero], axis=0)
        field = jnp.concatenate([image[t, :, :c] for t in range(count)], axis=0)
        wgrad_products(lhs, [cot], [field], acc, width)
        owners, _, each, _ = parts.shape
        for d in range(owners):
            block = acc[:, d * each : (d + 1) * each, :]
            parts[d] = block.astype(BF)

            @pl.when(ids[0] == d)
            def _():
                own[...] = block

    return body


def image_wgrad(ids, image, c, owners, width):
    count, n, wide = image.shape
    w = wide - c
    each = w // owners
    return pl.pallas_call(
        image_kernel(width),
        out_shape=[
            jax.ShapeDtypeStruct((9, each, c), F32),
            jax.ShapeDtypeStruct((owners, 9, each, c), BF),
        ],
        in_specs=[SM, VM],
        out_specs=[VM, VM],
        scratch_shapes=[pltpu.VMEM((9 * w, count * n), BF), pltpu.VMEM((9, w, c), F32)],
        compiler_params=PARAMS,
        name="image_wgrad",
    )(ids, image)


def strips_summed(keep, send):
    total = keep + swap(send, "dp", 1)
    owned, c = total.shape[1:]
    count = lax.axis_size("space")
    at = lax.axis_index("space")
    blocks = total.reshape(9, count, owned // count, c)
    mine = lax.dynamic_index_in_dim(blocks, at, 1, keepdims=False)
    for k in range(1, count):
        sent = lax.dynamic_index_in_dim(blocks, at ^ k, 1, keepdims=False).astype(BF)
        mine = mine + swap(sent, "space", k).astype(F32)
    return mine.astype(BF)


def strips_gathered(mine):
    count = lax.axis_size("space")
    at = lax.axis_index("space")
    _, each, c = mine.shape
    got = jnp.stack([mine] + [swap(mine, "space", k) for k in range(1, count)])
    whole = jnp.stack(
        [lax.dynamic_index_in_dim(got, at ^ j, 0, keepdims=False) for j in range(count)]
    )
    return whole.transpose(0, 2, 1, 3).reshape(count * each, 3, 3, c).astype(F32)


def images_summed(own, parts):
    owners = parts.shape[0]
    got = lax.all_to_all(parts, "dp", 0, 0)
    here = (jnp.arange(owners) == lax.axis_index("dp"))[:, None, None, None]
    return jnp.sum(jnp.where(here, own, got.astype(F32)), axis=0).astype(BF)


def strips_shared(mine):
    count = lax.axis_size("space")
    whole = lax.all_to_all(jnp.broadcast_to(mine, (count,) + mine.shape), "space", 0, 0)
    _, taps, each, c = whole.shape
    whole = whole.transpose(0, 2, 1, 3).reshape(count * each, 3, 3, c)
    return whole.astype(F32)


def after(value, *others):
    return lax.optimization_barrier((value,) + others)[0]


def per_device(inputs, pre_act, grad_out, w_first, w_second):
    _, height, width, c = inputs.shape
    n = height * width
    dp = lax.axis_size("dp")
    chips = dp // 2
    owned = w_first.shape[0]
    me = lax.axis_index("dp")
    strips = lax.axis_size("space")
    at = lax.axis_index("space")
    ids = jnp.stack([me, at, strips - 1 - at]).astype(jnp.int32)

    same_core = [[2 * q + k for q in range(chips)] for k in range(2)]

    def sent_to_chips(rows):
        return [swap(rows, "dp", k) for k in range(2, dp, 2)]

    def sent_to_pair(shards):
        return [shard for own in shards for shard in (own, swap(own, "dp", 1))]

    x = inputs.reshape(n, c)
    h = pre_act.reshape(n, c)
    g = grad_out.reshape(n, c)

    w2 = w_second.reshape(owned, 9 * c)
    ready = prepared(h, g, dp, strips)

    down_pairs = [(i, i + 1) for i in range(strips - 1)]
    up_pairs = [(i + 1, i) for i in range(strips - 1)]
    tail = jnp.concatenate([g[n - 2 * width :], h[n - width :]], axis=0)
    head = jnp.concatenate([g[: 2 * width], h[:width]], axis=0)
    above = lax.ppermute(tail, "space", down_pairs)
    below = lax.ppermute(head, "space", up_pairs)
    w2, ready, above, below = lax.optimization_barrier((w2, ready, above, below))
    image = lax.all_to_all(ready, "space", 0, 0)
    w2_shards = lax.optimization_barrier([w2] + sent_to_chips(w2))
    shards = sent_to_pair(w2_shards)
    gup, hup = above[: 2 * width], above[2 * width :]
    gdown, hdown = below[: 2 * width], below[2 * width :]

    xs = [x] + sent_to_chips(after(x, *w2_shards[1:]))

    pre_ext, pieces = gated(ids, gup, g, gdown, hup, h, hdown, shards, width, chips)
    pieces, image = lax.optimization_barrier((pieces, image))
    image = after(image, *xs[1:])
    p_cots = lax.all_to_all(pieces, "dp", 0, 0, axis_index_groups=same_core)
    own, parts = image_wgrad(ids, image, c, dp, width)
    p_cots, own = lax.optimization_barrier((p_cots, own))
    mine = strips_summed(*strip_wgrad(ids, xs, p_cots, width))
    share = images_summed(own, after(parts, p_cots))

    w1 = w_first.reshape(owned, 9 * c)
    w1_shards = [w1] + sent_to_chips(after(w1, share))
    w1_shards = sent_to_pair(w1_shards)
    first = strips_gathered(mine)
    second = strips_shared(share)
    in_grad = plain(ids, pre_ext, w1_shards, width)
    return in_grad.reshape(inputs.shape), first, second


def solution(mesh):
    return jax.shard_map(
        per_device,
        mesh=mesh,
        in_specs=(
            P("dp", "space", None, None),
            P("dp", "space", None, None),
            P("dp", "space", None, None),
            P("dp", None, None, None),
            P("dp", None, None, None),
        ),
        out_specs=(
            P("dp", "space", None, None),
            P("dp", None, None, None),
            P("dp", None, None, None),
        ),
        check_vma=False,
    )
```

```python
import jax
import jax.numpy as jnp
from jax import lax
from jax.experimental import pallas as pl
from jax.experimental.pallas import tpu as pltpu
from jax.sharding import PartitionSpec as P

BF = jnp.bfloat16
F32 = jnp.float32
PARAMS = pltpu.CompilerParams(vmem_limit_bytes=48 * 1024 * 1024)
ANY = pl.BlockSpec(memory_space=pltpu.HBM)
VM = pl.BlockSpec(memory_space=pltpu.VMEM)
SM = pl.BlockSpec(memory_space=pltpu.SMEM)


def xor_pairs(count, k):
    return [(i, i ^ k) for i in range(count)]


def swap(value, axis, k):
    return lax.ppermute(value, axis, xor_pairs(lax.axis_size(axis), k))


def shifted(flat, width):
    rows = flat.shape[0]
    wide = flat.astype(F32)
    col = lax.broadcasted_iota(jnp.int32, wide.shape, 0) % width
    left = jnp.where(col == 0, 0.0, pltpu.roll(wide, 1, 0)).astype(BF)
    right = jnp.where(col == width - 1, 0.0, pltpu.roll(wide, rows - 1, 0)).astype(BF)
    return left, flat, right


def products(field, kernel, copies, n, c, width):
    acc = None
    for r in range(3):
        for copy in copies[r]:
            copy.wait()
        for s in range(3):
            tap = 3 * r + s
            lhs = field[s, (2 - r) * width : (2 - r) * width + n, :]
            part = jnp.dot(lhs, kernel[:, tap * c : (tap + 1) * c], preferred_element_type=F32)
            acc = part if acc is None else acc + part
    return acc


def in_hbm(arrays):
    return [pltpu.with_memory_space_constraint(array, pltpu.HBM) for array in arrays]


def prep_kernel(owners, strips):
    def body(h, g, out):
        n, c = h.shape
        each = c // (strips * owners)
        src = lax.broadcasted_iota(jnp.int32, (c, c), 0)
        dst = lax.broadcasted_iota(jnp.int32, (c, c), 1)
        owner, rest = src // (strips * each), src % (strips * each)
        goes = (rest // each) * (owners * each) + owner * each + rest % each
        moved = jnp.dot(g[...], (goes == dst).astype(BF), preferred_element_type=F32).astype(BF)
        hf = h[...].astype(F32)
        act = (hf * jax.nn.sigmoid(hf)).astype(BF)
        w = c // strips
        for t in range(strips):
            out[t, :, :c] = act
            out[t, :, c:] = moved[:, t * w : (t + 1) * w]

    return body


def prepared(h, g, owners, strips):
    n, c = h.shape
    return pl.pallas_call(
        prep_kernel(owners, strips),
        out_shape=jax.ShapeDtypeStruct((strips, n, c + c // strips), BF),
        in_specs=[VM, VM],
        out_specs=VM,
        compiler_params=PARAMS,
        name="prepared",
    )(h, g)


def weight_copies(ids, weights, kernel, sems):
    count = len(weights)
    rows, wide = weights[0].shape
    copies = []
    for r in range(3):
        cols = pl.ds(r * (wide // 3), wide // 3)
        for k, weight in enumerate(weights):
            start = pl.multiple_of((ids[0] ^ k) * rows, rows)
            copies.append(
                pltpu.make_async_copy(
                    weight.at[:, cols], kernel.at[pl.ds(start, rows), cols], sems.at[r * count + k]
                )
            )
            copies[-1].start()
    return [copies[r * count : (r + 1) * count] for r in range(3)]


def gated_kernel(count, width):
    def body(*refs):
        ids, gup, g, gdown, hup, h, hdown = refs[:7]
        weights = refs[7 : 7 + count]
        out, parts, field, kernel, sems = refs[7 + count :]
        copies = weight_copies(ids, weights, kernel, sems)
        left, same, right = shifted(
            jnp.concatenate([gup[...], g[...], gdown[...]], axis=0), width
        )
        field[0] = right
        field[1] = same
        field[2] = left
        n, c = out.shape
        acc = products(field, kernel, copies, n, c, width)
        hf = jnp.concatenate([hup[...], h[...], hdown[...]], axis=0).astype(F32)
        sig = jax.nn.sigmoid(hf)
        acc = acc * (sig * (1.0 + hf * (1.0 - sig)))
        row = lax.broadcasted_iota(jnp.int32, acc.shape, 0)
        inside = jnp.logical_and(
            jnp.logical_or(row >= width, ids[1] > 0),
            jnp.logical_or(row < n - width, ids[2] > 0),
        )
        res = jnp.where(inside, acc, 0.0).astype(BF)
        out[...] = res
        chips = parts.shape[0]
        w = c // chips
        for t in range(chips):
            parts[t] = res[:, t * w : (t + 1) * w]

    return body


def gated(ids, gup, g, gdown, hup, h, hdown, weights, width, pieces):
    n, c = h.shape
    count = len(weights)
    rows = n + 2 * width
    return pl.pallas_call(
        gated_kernel(count, width),
        out_shape=[
            jax.ShapeDtypeStruct((rows, c), BF),
            jax.ShapeDtypeStruct((pieces, rows, c // pieces), BF),
        ],
        in_specs=[SM] + [VM] * 6 + [ANY] * count,
        out_specs=[VM, VM],
        scratch_shapes=[
            pltpu.VMEM((3, rows + 2 * width, c), BF),
            pltpu.VMEM((weights[0].shape[0] * count, weights[0].shape[1]), BF),
            pltpu.SemaphoreType.DMA((3 * count,)),
        ],
        compiler_params=PARAMS,
        name="gated",
    )(ids, gup, g, gdown, hup, h, hdown, *in_hbm(weights))


def plain_kernel(count, width):
    def body(*refs):
        ids, ext = refs[:2]
        weights = refs[2 : 2 + count]
        out, field, kernel, sems = refs[2 + count :]
        copies = weight_copies(ids, weights, kernel, sems)
        left, same, right = shifted(ext[...], width)
        field[0] = right
        field[1] = same
        field[2] = left
        n, c = out.shape
        out[...] = products(field, kernel, copies, n, c, width)

    return body


def plain(ids, ext, weights, width):
    rows, c = ext.shape
    count = len(weights)
    return pl.pallas_call(
        plain_kernel(count, width),
        out_shape=jax.ShapeDtypeStruct((rows - 2 * width, c), F32),
        in_specs=[SM, VM] + [ANY] * count,
        out_specs=VM,
        scratch_shapes=[
            pltpu.VMEM((3, rows, c), BF),
            pltpu.VMEM((weights[0].shape[0] * count, weights[0].shape[1]), BF),
            pltpu.SemaphoreType.DMA((3 * count,)),
        ],
        compiler_params=PARAMS,
        name="plain",
    )(ids, ext, *in_hbm(weights))


def wgrad_products(lhs, cots, fields, acc, width):
    w = cots[0].shape[1]
    n = cots[0].shape[0] - 2 * width
    for i, cot in enumerate(cots):
        left, same, right = shifted(cot, width)
        for s, part in enumerate((right, same, left)):
            for r in range(3):
                tap = 3 * r + s
                lhs[tap * w : (tap + 1) * w, i * n : (i + 1) * n] = part[
                    (2 - r) * width : (2 - r) * width + n, :
                ].T
    for tap in range(9):
        total = None
        for i, field in enumerate(fields):
            part = jnp.dot(
                lhs[tap * w : (tap + 1) * w, i * n : (i + 1) * n],
                field[...],
                preferred_element_type=F32,
            )
            total = part if total is None else total + part
        acc[tap] = total


def strip_kernel(count, width):
    def body(*refs):
        ids = refs[0]
        fields = refs[1 : 1 + count]
        cots, keep, send, lhs, acc = refs[1 + count :]
        ordered = [cots[(ids[0] >> 1) ^ i] for i in range(count)]
        wgrad_products(lhs, ordered, fields, acc, width)
        half = keep.shape[1]
        mine = ids[0] & 1
        keep[...] = acc[:, pl.ds(pl.multiple_of(mine * half, half), half), :]
        send[...] = acc[:, pl.ds(pl.multiple_of((1 - mine) * half, half), half), :]

    return body


def strip_wgrad(ids, fields, cots, width):
    count = len(fields)
    n, c = fields[0].shape
    w = cots.shape[2]
    half = jax.ShapeDtypeStruct((9, w // 2, c), F32)
    return pl.pallas_call(
        strip_kernel(count, width),
        out_shape=[half, half],
        in_specs=[SM] + [VM] * (count + 1),
        out_specs=[VM, VM],
        scratch_shapes=[pltpu.VMEM((9 * w, count * n), BF), pltpu.VMEM((9, w, c), F32)],
        compiler_params=PARAMS,
        name="strip_wgrad",
    )(ids, *fields, cots)


def image_kernel(width):
    def body(ids, image, own, parts, lhs, acc):
        count, n, _ = image.shape
        c = own.shape[2]
        zero = jnp.zeros((width, acc.shape[1]), BF)
        cot = jnp.concatenate([zero] + [image[t, :, c:] for t in range(count)] + [zero], axis=0)
        field = jnp.concatenate([image[t, :, :c] for t in range(count)], axis=0)
        wgrad_products(lhs, [cot], [field], acc, width)
        owners, _, each, _ = parts.shape
        for d in range(owners):
            block = acc[:, d * each : (d + 1) * each, :]
            parts[d] = block.astype(BF)

            @pl.when(ids[0] == d)
            def _():
                own[...] = block

    return body


def image_wgrad(ids, image, c, owners, width):
    count, n, wide = image.shape
    w = wide - c
    each = w // owners
    return pl.pallas_call(
        image_kernel(width),
        out_shape=[
            jax.ShapeDtypeStruct((9, each, c), F32),
            jax.ShapeDtypeStruct((owners, 9, each, c), BF),
        ],
        in_specs=[SM, VM],
        out_specs=[VM, VM],
        scratch_shapes=[pltpu.VMEM((9 * w, count * n), BF), pltpu.VMEM((9, w, c), F32)],
        compiler_params=PARAMS,
        name="image_wgrad",
    )(ids, image)


def strips_summed(keep, send):
    total = keep + swap(send, "dp", 1)
    owned, c = total.shape[1:]
    count = lax.axis_size("space")
    at = lax.axis_index("space")
    blocks = total.reshape(9, count, owned // count, c)
    mine = lax.dynamic_index_in_dim(blocks, at, 1, keepdims=False)
    for k in range(1, count):
        sent = lax.dynamic_index_in_dim(blocks, at ^ k, 1, keepdims=False).astype(BF)
        mine = mine + swap(sent, "space", k).astype(F32)
    return mine.astype(BF)


def strips_gathered(mine):
    count = lax.axis_size("space")
    at = lax.axis_index("space")
    _, each, c = mine.shape
    got = jnp.stack([mine] + [swap(mine, "space", k) for k in range(1, count)])
    whole = jnp.stack(
        [lax.dynamic_index_in_dim(got, at ^ j, 0, keepdims=False) for j in range(count)]
    )
    return whole.transpose(0, 2, 1, 3).reshape(count * each, 3, 3, c).astype(F32)


def images_summed(own, parts):
    owners = parts.shape[0]
    got = lax.all_to_all(parts, "dp", 0, 0)
    here = (jnp.arange(owners) == lax.axis_index("dp"))[:, None, None, None]
    return jnp.sum(jnp.where(here, own, got.astype(F32)), axis=0).astype(BF)


def strips_shared(mine):
    count = lax.axis_size("space")
    whole = lax.all_to_all(jnp.broadcast_to(mine, (count,) + mine.shape), "space", 0, 0)
    _, taps, each, c = whole.shape
    whole = whole.transpose(0, 2, 1, 3).reshape(count * each, 3, 3, c)
    return whole.astype(F32)


def after(value, *others):
    return lax.optimization_barrier((value,) + others)[0]


def per_device(inputs, pre_act, grad_out, w_first, w_second):
    _, height, width, c = inputs.shape
    n = height * width
    dp = lax.axis_size("dp")
    chips = dp // 2
    owned = w_first.shape[0]
    me = lax.axis_index("dp")
    strips = lax.axis_size("space")
    at = lax.axis_index("space")
    ids = jnp.stack([me, at, strips - 1 - at]).astype(jnp.int32)

    same_core = [[2 * q + k for q in range(chips)] for k in range(2)]

    def sent_to_chips(rows):
        return [swap(rows, "dp", k) for k in range(2, dp, 2)]

    def sent_to_pair(shards):
        return [shard for own in shards for shard in (own, swap(own, "dp", 1))]

    x = inputs.reshape(n, c)
    h = pre_act.reshape(n, c)
    g = grad_out.reshape(n, c)

    w2 = w_second.reshape(owned, 9 * c)
    ready = prepared(h, g, dp, strips)

    down_pairs = [(i, i + 1) for i in range(strips - 1)]
    up_pairs = [(i + 1, i) for i in range(strips - 1)]
    tail = jnp.concatenate([g[n - 2 * width :], h[n - width :]], axis=0)
    head = jnp.concatenate([g[: 2 * width], h[:width]], axis=0)
    above = lax.ppermute(tail, "space", down_pairs)
    below = lax.ppermute(head, "space", up_pairs)
    w2, ready, above, below = lax.optimization_barrier((w2, ready, above, below))
    image = lax.all_to_all(ready, "space", 0, 0)
    w2_shards = [w2] + sent_to_chips(w2)
    shards = sent_to_pair(w2_shards)
    gup, hup = above[: 2 * width], above[2 * width :]
    gdown, hdown = below[: 2 * width], below[2 * width :]

    xs = [x] + sent_to_chips(after(x, w2_shards[1]))

    pre_ext, pieces = gated(ids, gup, g, gdown, hup, h, hdown, shards, width, chips)
    pieces, image = lax.optimization_barrier((pieces, image))
    image = after(image, *xs[1:])
    p_cots = lax.all_to_all(pieces, "dp", 0, 0, axis_index_groups=same_core)
    own, parts = image_wgrad(ids, image, c, dp, width)
    p_cots, own = lax.optimization_barrier((p_cots, own))
    mine = strips_summed(*strip_wgrad(ids, xs, p_cots, width))
    share = images_summed(own, after(parts, p_cots))

    w1 = w_first.reshape(owned, 9 * c)
    w1_shards = [w1] + sent_to_chips(after(w1, share))
    w1_shards = sent_to_pair(w1_shards)
    first = strips_gathered(mine)
    second = strips_shared(share)
    in_grad = plain(ids, pre_ext, w1_shards, width)
    return in_grad.reshape(inputs.shape), first, second


def solution(mesh):
    return jax.shard_map(
        per_device,
        mesh=mesh,
        in_specs=(
            P("dp", "space", None, None),
            P("dp", "space", None, None),
            P("dp", "space", None, None),
            P("dp", None, None, None),
            P("dp", None, None, None),
        ),
        out_specs=(
            P("dp", "space", None, None),
            P("dp", None, None, None),
            P("dp", None, None, None),
        ),
        check_vma=False,
    )
```
